256 devices in a mesh: chan: 16 (over x, y), tm: 16 (over z, core).
Axes of the slice: x: 4, y: 4, z: 8, core: 2. Of those that a mesh axis runs over, the one named last changes fastest.
Arguments:
- records: bfloat16 [16, 6144, 1536], P('tm', 'chan')
- partners: int32 [16, 3], P('chan'), may hold values from 0 to 15, as said below
- counts: int32 [16], P('chan'), may hold values from 1 to 3, as said below
- sources: int32 [16, 2], P('chan'), may hold values from 0 to 383, as said below
Outputs:
- xcorr: float32 [16, 384, 3, 2, 384], P('chan', 'tm')
The draws below stay inside these ranges and needn't reach their ends.
Inputs may be any that keep to these rules, and one draw needn't show every extreme that they name: `partners`: each row holds 3 different blocks. `counts`: some block has all 3 slots live. `sources`: each row holds 2 different channels.
All inputs are finite; a program needn't handle non-finite values.
Results may differ from the reference program's by a relative error of at most 0.008.
Values may be sent and summed in bfloat16 or wider, within the bound.
A program may use at most 64 MiB of HBM per device.

```python
import math
import jax
import jax.numpy as jnp
from jax import lax

CH = 384
L = 1536
F = 320
HL = 192
SMOOTH = 32
S = 2
P_SIZE = 3
NB = 16
NW = 16


def draw_records(key, part):
    keys = jax.random.split(key, 6)
    channels = NB * CH
    noise = jax.random.normal(keys[0], (NW, channels, L), jnp.float32)
    chan_scale = jnp.exp(jax.random.uniform(keys[1], (1, channels, 1), jnp.float32, 0.0, math.log(10.0)))
    win_scale = jnp.exp(jax.random.uniform(keys[2], (NW, 1, 1), jnp.float32, math.log(0.5), math.log(2.0)))
    tone_bin = jax.random.randint(keys[3], (1, channels, 1), 1, F + 1)
    tone_phase = jax.random.uniform(keys[4], (NW, channels, 1), jnp.float32, -math.pi, math.pi)
    tone_size = jax.random.uniform(keys[5], (1, channels, 1), jnp.float32, 0.0, 4.0)
    sample_index = jnp.arange(L, dtype=jnp.int32)[None, None, :]
    angle = (tone_bin * sample_index % L).astype(jnp.float32) * (2.0 * math.pi / L) + tone_phase
    signal = chan_scale * win_scale * (noise + tone_size * jnp.sin(angle))
    return signal.astype(jnp.bfloat16)


def shifted_rows(key, rows, total, picked):
    keys = jax.random.split(key, 2)
    row_keys = jax.random.split(keys[0], rows)
    perms = jax.vmap(lambda one_key: jax.random.permutation(one_key, total)[:picked])(row_keys)
    chosen = jax.random.randint(keys[1], (), 0, rows)
    row_index = jnp.arange(rows, dtype=jnp.int32)
    target = jnp.where(row_index == chosen, total - 1, jnp.where(row_index == (chosen + 1) % rows, 0, perms[:, 0]))
    return jnp.mod(perms - perms[:, :1] + target[:, None], total).astype(jnp.int32)


def draw_partners(key, part):
    return shifted_rows(jax.random.fold_in(key, 5), NB, NB, P_SIZE)


def draw_counts(key, part):
    keys = jax.random.split(key, 2)
    values = jax.random.randint(keys[0], (NB,), 1, P_SIZE + 1)
    chosen = jax.random.randint(keys[1], (), 0, NB)
    values = values.at[(chosen + 1) % NB].set(1)
    return values.at[chosen].set(P_SIZE).astype(jnp.int32)


def draw_sources(key, part):
    return shifted_rows(jax.random.fold_in(key, 11), NB, CH, S)


def setup_inputs(seed: int = 0) -> dict:
    arg_keys = jax.random.split(jax.random.key(seed), 5)
    records = draw_records(jax.random.fold_in(arg_keys[4], 71), 0)
    partners = draw_partners(jax.random.fold_in(arg_keys[4], 71), 0)
    counts = draw_counts(jax.random.fold_in(arg_keys[4], 71), 0)
    sources = draw_sources(jax.random.fold_in(arg_keys[4], 71), 0)
    return {"records": records, "partners": partners, "counts": counts, "sources": sources}


def dft_table(length, bins):
    sample_index = jnp.arange(length, dtype=jnp.int32)[:, None]
    bin_index = jnp.arange(bins, dtype=jnp.int32)[None, :] + 1
    phase_index = sample_index * bin_index % length
    angle = phase_index.astype(jnp.float32) * (2.0 * math.pi / length)
    return jnp.concatenate([jnp.cos(angle), -jnp.sin(angle)], axis=1).astype(jnp.bfloat16)

def lag_table(length, bins, half):
    bin_index = jnp.arange(bins, dtype=jnp.int32)[:, None] + 1
    lag_index = jnp.arange(2 * half, dtype=jnp.int32)[None, :] - half
    phase_index = jnp.mod(bin_index * lag_index, length)
    angle = phase_index.astype(jnp.float32) * (2.0 * math.pi / length)
    return jnp.concatenate([jnp.cos(angle), -jnp.sin(angle)], axis=0)

def band_table(bins, half):
    input_bin = jnp.arange(bins, dtype=jnp.int32)[:, None]
    output_bin = jnp.arange(bins, dtype=jnp.int32)[None, :]
    centre = jnp.clip(output_bin, half, bins - 1 - half)
    return (jnp.abs(input_bin - centre) <= half).astype(jnp.float32)

def whiten(block_records):
    windows, channels, length = block_records.shape
    signal = block_records.astype(jnp.float32)
    signal = signal - lax.optimization_barrier(jnp.mean(signal, axis=-1, keepdims=True))
    demeaned = signal.astype(jnp.bfloat16).reshape(windows * channels, length)
    spectrum = jnp.dot(demeaned, dft_table(L, F), preferred_element_type=jnp.float32)
    real_part = spectrum[:, :F]
    imag_part = spectrum[:, F:]
    amplitude = jnp.sqrt(real_part * real_part + imag_part * imag_part)
    smooth = jnp.dot(amplitude, band_table(F, SMOOTH), precision=lax.Precision.HIGHEST) / (2 * SMOOTH + 1)
    factor = 1.0 / (smooth + 1e-06)
    whitened = jnp.concatenate([real_part * factor, imag_part * factor], axis=1)
    return whitened.astype(jnp.bfloat16).reshape(windows, channels, 2 * F)

def reference(records, partners, counts, sources):
    by_block = records.reshape(NW, NB, CH, L).transpose(1, 0, 2, 3)
    white = lax.map(whiten, by_block)
    inverse = lag_table(L, F, HL)
    scale = 1.0 / math.sqrt(F * NW)

    def one_block(block):
        own = white[block]
        source_spec = jnp.take(own, sources[block], axis=1).astype(jnp.float32)
        partner_spec = jnp.take(white, partners[block], axis=0).astype(jnp.float32)
        live = (jnp.arange(P_SIZE, dtype=jnp.int32) < counts[block]).astype(jnp.float32)
        src_real = source_spec[..., :F]
        src_imag = source_spec[..., F:]
        rec_real = partner_spec[..., :F]
        rec_imag = partner_spec[..., F:]
        cross_real = jnp.einsum('wsf,pwcf->cpsf', src_real, rec_real) + jnp.einsum('wsf,pwcf->cpsf', src_imag, rec_imag)
        cross_imag = jnp.einsum('wsf,pwcf->cpsf', src_real, rec_imag) - jnp.einsum('wsf,pwcf->cpsf', src_imag, rec_real)
        stacked = jnp.concatenate([cross_real, cross_imag], axis=-1) * live[None, :, None, None]
        lagged = jnp.dot(stacked.reshape(CH * P_SIZE * S, 2 * F), inverse, precision=lax.Precision.HIGHEST)
        return lagged.reshape(CH, P_SIZE, S, 2 * HL) * scale
    return lax.map(one_block, jnp.arange(NB, dtype=jnp.int32))
```

```python
import functools
import math

import jax
import jax.numpy as jnp
import ml_dtypes
import numpy as np
from jax import lax
from jax.experimental import pallas as pl
from jax.experimental.pallas import tpu as pltpu
from jax.sharding import PartitionSpec as P

L = 1536
F = 320
HL = 192
SMOOTH = 32
ROWS = 8
LANES = 128
FULL = 256
HALF = F - FULL
COLS = 2 * F
MESH = pl.DeviceIdType.MESH


def tables():
    sample_index = np.arange(L, dtype=np.int64)[:, None]
    bin_index = np.arange(F, dtype=np.int64)[None, :] + 1
    phase_index = sample_index * bin_index % L
    angle = phase_index.astype(np.float32) * np.float32(2.0 * math.pi / L)
    cosine, sine = np.cos(angle), -np.sin(angle)
    table = np.concatenate(
        [cosine[:, :FULL], sine[:, :FULL], cosine[:, FULL:], sine[:, FULL:]], axis=1
    ).astype(np.float32)
    high = table.astype(ml_dtypes.bfloat16)
    lag_rows = np.concatenate([np.arange(L - HL, L), np.arange(HL)])
    low = (table - high.astype(np.float32)).astype(ml_dtypes.bfloat16)[lag_rows]
    return high, low


def dot(left, right):
    return jnp.dot(left, right, preferred_element_type=jnp.float32)


def dot_rows(left, right):
    return lax.dot_general(left, right, (((1,), (1,)), ((), ())), preferred_element_type=jnp.float32)


def split(value):
    high = value.astype(jnp.bfloat16)
    return high, (value - high.astype(jnp.float32)).astype(jnp.bfloat16)


def band_matrix():
    width = FULL + LANES
    row = lax.broadcasted_iota(jnp.int32, (width, width), 0)
    col = lax.broadcasted_iota(jnp.int32, (width, width), 1)
    out_bin = jnp.where(col < F, col, col - HALF)
    centre = jnp.clip(out_bin, SMOOTH, F - 1 - SMOOTH)
    near = (jnp.abs(row - centre) <= SMOOTH) & (row < F)
    return jnp.where(near, 1.0, 0.0).astype(jnp.bfloat16)


def whiten(signal, table, band):
    mean = jnp.sum(signal, axis=1, keepdims=True) * (1.0 / L)
    spectrum = dot((signal - mean).astype(jnp.bfloat16), table)
    real, imag, mixed = spectrum[:, :FULL], spectrum[:, FULL : 2 * FULL], spectrum[:, 2 * FULL :]
    squares = mixed * mixed
    power = jnp.concatenate([real * real + imag * imag, squares + pltpu.roll(squares, HALF, 1)], axis=1)
    amplitude = jnp.sqrt(power)
    first, rest = split(amplitude)
    second, third = split(amplitude - first.astype(jnp.float32))
    smooth = (dot(first, band) + dot(second, band) + dot(third, band)) / (2 * SMOOTH + 1)
    factor = 1.0 / (smooth + 1e-06)
    return jnp.concatenate(
        [real * factor[:, :FULL], imag * factor[:, :FULL], mixed * factor[:, FULL:]], axis=1
    )


def kernel(
    dims,
    rec_hbm,
    table_hbm,
    low_hbm,
    partners_ref,
    counts_ref,
    sources_ref,
    out_ref,
    rec,
    table,
    lag_high,
    lag_low,
    band,
    white_send,
    white_recv,
    near_send,
    near_recv,
    near_rows,
    far_send,
    far_recv,
    source_rows,
    partner_rows,
    cross,
    stack_send,
    stack_recvs,
    local_sems,
    near_sems,
    far_sems,
    white_sems,
    stack_sems,
):
    blocks, shares, pieces, slots, sources = dims
    me_chan, me_tm = lax.axis_index("chan"), lax.axis_index("tm")

    def others(axis, me, size):
        return [(axis, lax.rem(me + step, size)) for step in range(1, size)]

    tm_peers = others("tm", me_tm, shares)
    chan_peers = others("chan", me_chan, blocks)

    barrier = pltpu.get_barrier_semaphore()
    for axis, peer in tm_peers + chan_peers:
        pl.semaphore_signal(barrier, inc=1, device_id={axis: peer}, device_id_type=MESH)

    loads = [pltpu.make_async_copy(rec_hbm.at[:, piece], rec.at[piece], local_sems.at[piece]) for piece in range(pieces)]
    table_load = pltpu.make_async_copy(table_hbm, table, local_sems.at[pieces])
    lag_loads = [
        pltpu.make_async_copy(table_hbm.at[pl.ds(L - HL, HL)], lag_high.at[pl.ds(0, HL)], local_sems.at[pieces + 1]),
        pltpu.make_async_copy(table_hbm.at[pl.ds(0, HL)], lag_high.at[pl.ds(HL, HL)], local_sems.at[pieces + 2]),
        pltpu.make_async_copy(low_hbm, lag_low, local_sems.at[pieces + 3]),
    ]
    for copy in loads + [table_load] + lag_loads:
        copy.start()

    def send(src, dst, sems, peer):
        axis, index = peer
        pltpu.make_async_remote_copy(
            src_ref=src, dst_ref=dst, send_sem=sems[0], recv_sem=sems[1], device_id={axis: index}, device_id_type=MESH
        ).start()

    def wait_bytes(ref, sem):
        pltpu.make_async_copy(ref, ref, sem).wait()

    band[...] = band_matrix()
    for copy in loads:
        copy.wait()

    row_id = lax.broadcasted_iota(jnp.int32, (ROWS, L), 0)
    picked = []
    for source in range(sources):
        channel = sources_ref[source]
        share = lax.div(channel, pieces * ROWS)
        within = channel - share * (pieces * ROWS)
        piece = lax.div(within, ROWS)
        tile = rec[piece, share].astype(jnp.float32)
        picked.append(jnp.sum(jnp.where(row_id == within - piece * ROWS, tile, 0.0), axis=0, keepdims=True))
    head_id = lax.broadcasted_iota(jnp.int32, (2 * ROWS, L), 0)
    head = jnp.broadcast_to(picked[0], (2 * ROWS, L))
    for source in range(1, sources):
        head = jnp.where(head_id == source, picked[source], head)

    table_load.wait()
    for piece in range(pieces):
        signal = rec[piece].astype(jnp.float32).reshape(shares * ROWS, L)
        if piece == 0:
            signal = jnp.concatenate([head, signal], axis=0)
        white = whiten(signal, table[...], band[...])
        if piece == 0:
            near_send[...] = white[:sources].astype(jnp.bfloat16).astype(jnp.float32)
            near_recv[me_tm] = near_send[...]
            white = white[2 * ROWS :]
        white = white.reshape(shares, ROWS, COLS).astype(jnp.bfloat16)
        white_send[piece] = white
        white_recv[piece, me_tm] = white_send[piece, me_tm]
        if piece == 0:
            pl.semaphore_wait(barrier, len(tm_peers) + len(chan_peers))
            for peer in tm_peers:
                send(near_send, near_recv.at[me_tm], (near_sems.at[0], near_sems.at[1]), peer)
        for peer in tm_peers:
            send(
                white_send.at[piece, peer[1]],
                white_recv.at[piece, me_tm],
                (white_sems.at[0, piece], white_sems.at[1, piece]),
                peer,
            )

    wait_bytes(near_recv.at[pl.ds(0, shares - 1)], near_sems.at[1])
    for window in range(shares):
        near_rows[pl.ds(window * sources, sources), :] = near_recv[window]
    far_send[...] = near_rows[...].astype(jnp.bfloat16)
    far_recv[me_chan] = far_send[...]
    for peer in chan_peers:
        send(far_send, far_recv.at[me_chan], (far_sems.at[0], far_sems.at[1]), peer)
    wait_bytes(far_recv.at[pl.ds(0, blocks - 1)], far_sems.at[1])
    for tile in range(COLS // LANES):
        source_rows[:, tile] = far_recv[:, :, pl.ds(tile * LANES, LANES)].astype(jnp.float32)

    for copy in lag_loads:
        copy.wait()
    lane = lax.broadcasted_iota(jnp.int32, (ROWS, LANES), 1)
    scale = 1.0 / math.sqrt(F * shares)

    for piece in range(pieces):
        wait_bytes(white_recv.at[piece, pl.ds(0, shares - 1)], white_sems.at[1, piece])
        spectra = white_recv[piece].astype(jnp.float32)
        partner_rows[:, :, :COLS] = spectra
        partner_rows[:, :, COLS:] = pltpu.roll(spectra[:, :, 2 * FULL :], HALF, 2)

        def per_block(block, carry):
            def source_tile(window, source, tile):
                return source_rows[block, tile, pl.ds(window * sources + source, ROWS, stride=0), :]

            def partner_tile(window, tile):
                return partner_rows[window, :, pl.ds(tile * LANES, LANES)]

            tiles = FULL // LANES
            for tile in range(tiles):
                real, imag = [0.0] * sources, [0.0] * sources
                for window in range(shares):
                    b_re, b_im = partner_tile(window, tile), partner_tile(window, tiles + tile)
                    for source in range(sources):
                        a_re = source_tile(window, source, tile)
                        a_im = source_tile(window, source, tiles + tile)
                        real[source] = real[source] + (a_re * b_re + a_im * b_im)
                        imag[source] = imag[source] + (a_re * b_im - a_im * b_re)
                for source in range(sources):
                    cross[block * sources + source, :, pl.ds(tile * LANES, LANES)] = real[source]
                    cross[block * sources + source, :, pl.ds((tiles + tile) * LANES, LANES)] = imag[source]
            same, other = [0.0] * sources, [0.0] * sources
            for window in range(shares):
                b_mix, b_swap = partner_tile(window, 2 * tiles), partner_tile(window, 2 * tiles + 1)
                for source in range(sources):
                    a_mix = source_tile(window, source, 2 * tiles)
                    same[source] = same[source] + a_mix * b_mix
                    other[source] = other[source] + a_mix * b_swap
            for source in range(sources):
                real_part = same[source] + pltpu.roll(same[source], HALF, 1)
                imag_part = pltpu.roll(other[source], HALF, 1) - other[source]
                cross[block * sources + source, :, pl.ds(2 * FULL, LANES)] = jnp.where(
                    lane < HALF, real_part, imag_part
                )
            return carry

        lax.fori_loop(0, blocks, per_block, 0)
        high, low = split(cross[...].reshape(blocks * sources * ROWS, COLS))
        lagged = dot_rows(high, lag_high[...]) + dot_rows(low, lag_high[...]) + dot_rows(high, lag_low[...])
        stack_send[piece] = (lagged * scale).reshape(blocks, sources, ROWS, 2 * HL).astype(jnp.bfloat16)
        stack_recvs[piece][me_chan] = stack_send[piece, me_chan]
        for peer in chan_peers:
            send(
                stack_send.at[piece, peer[1]],
                stack_recvs[piece].at[me_chan],
                (stack_sems.at[0, piece], stack_sems.at[1, piece]),
                peer,
            )

    for piece in range(pieces):
        wait_bytes(stack_recvs[piece].at[pl.ds(0, blocks - 1)], stack_sems.at[1, piece])
        for slot in range(slots):
            stack = stack_recvs[piece][partners_ref[slot]].astype(jnp.float32)
            out_ref[slot, :, pl.ds(piece * ROWS, ROWS), :] = jnp.where(slot < counts_ref[0], stack, 0.0)

    wait_bytes(near_recv.at[pl.ds(0, shares - 1)], near_sems.at[0])
    wait_bytes(far_recv.at[pl.ds(0, blocks - 1)], far_sems.at[0])
    for piece in range(pieces):
        wait_bytes(white_recv.at[piece, pl.ds(0, shares - 1)], white_sems.at[0, piece])
        wait_bytes(stack_recvs[piece].at[pl.ds(0, blocks - 1)], stack_sems.at[0, piece])


def local(blocks, shares, records, partners, counts, sources):
    channels = records.shape[1]
    slots, picks = partners.shape[1], sources.shape[1]
    pieces = channels // (shares * ROWS)
    high, low = tables()
    any_spec = pl.BlockSpec(memory_space=pl.ANY)
    smem_spec = pl.BlockSpec(memory_space=pltpu.SMEM)
    bf16, f32 = jnp.bfloat16, jnp.float32
    result = pl.pallas_call(
        functools.partial(kernel, (blocks, shares, pieces, slots, picks)),
        out_shape=jax.ShapeDtypeStruct((slots, picks, pieces * ROWS, 2 * HL), f32),
        in_specs=[any_spec] * 3 + [smem_spec] * 3,
        out_specs=pl.BlockSpec(memory_space=pltpu.VMEM),
        scratch_shapes=[
            pltpu.VMEM((pieces, shares, ROWS, L), bf16),
            pltpu.VMEM((L, COLS), bf16),
            pltpu.VMEM((2 * HL, COLS), bf16),
            pltpu.VMEM((2 * HL, COLS), bf16),
            pltpu.VMEM((FULL + LANES, FULL + LANES), bf16),
            pltpu.VMEM((pieces, shares, ROWS, COLS), bf16),
            pltpu.VMEM((pieces, shares, ROWS, COLS), bf16),
            pltpu.VMEM((picks, COLS), f32),
            pltpu.VMEM((shares, picks, COLS), f32),
            pltpu.VMEM((shares * picks, COLS), f32),
            pltpu.VMEM((shares * picks, COLS), bf16),
            pltpu.VMEM((blocks, shares * picks, COLS), bf16),
            pltpu.VMEM((blocks, COLS // LANES, shares * picks, LANES), f32),
            pltpu.VMEM((shares, ROWS, COLS + LANES), f32),
            pltpu.VMEM((blocks * picks, ROWS, COLS), f32),
            pltpu.VMEM((pieces, blocks, picks, ROWS, 2 * HL), bf16),
            [pltpu.VMEM((blocks, picks, ROWS, 2 * HL), bf16) for _ in range(pieces)],
            pltpu.SemaphoreType.DMA((pieces + 4,)),
            pltpu.SemaphoreType.DMA((2,)),
            pltpu.SemaphoreType.DMA((2,)),
            pltpu.SemaphoreType.DMA((2, pieces)),
            pltpu.SemaphoreType.DMA((2, pieces)),
        ],
        compiler_params=pltpu.CompilerParams(
            collective_id=0, has_side_effects=True, vmem_limit_bytes=48 * 1024 * 1024
        ),
        name="correlate",
    )(
        records.reshape(shares, pieces, ROWS, L),
        jnp.asarray(high),
        jnp.asarray(low),
        partners.reshape(slots),
        counts,
        sources.reshape(picks),
    )
    return result.transpose(2, 0, 1, 3)[None]


def solution(mesh):
    return jax.shard_map(
        functools.partial(local, mesh.shape["chan"], mesh.shape["tm"]),
        mesh=mesh,
        in_specs=(P("tm", "chan", None), P("chan", None), P("chan"), P("chan", None)),
        out_specs=P("chan", "tm", None, None, None),
        check_vma=False,
    )
```

```python
import functools
import math

import jax
import jax.numpy as jnp
import ml_dtypes
import numpy as np
from jax import lax
from jax.experimental import pallas as pl
from jax.experimental.pallas import tpu as pltpu
from jax.sharding import PartitionSpec as P

L = 1536
F = 320
HL = 192
SMOOTH = 32
ROWS = 8
LANES = 128
FULL = 256
HALF = F - FULL
COLS = 2 * F
CORES = 2
TOGETHER = 2
MESH = pl.DeviceIdType.MESH


def tables():
    sample_index = np.arange(L, dtype=np.int64)[:, None]
    bin_index = np.arange(F, dtype=np.int64)[None, :] + 1
    phase_index = sample_index * bin_index % L
    angle = phase_index.astype(np.float32) * np.float32(2.0 * math.pi / L)
    cosine, sine = np.cos(angle), -np.sin(angle)
    table = np.concatenate(
        [cosine[:, :FULL], sine[:, :FULL], cosine[:, FULL:], sine[:, FULL:]], axis=1
    ).astype(np.float32)
    high = table.astype(ml_dtypes.bfloat16)
    lag_rows = np.concatenate([np.arange(L - HL, L), np.arange(HL)])
    low = (table - high.astype(np.float32)).astype(ml_dtypes.bfloat16)[lag_rows]
    return high, low


def dot(left, right):
    return jnp.dot(left, right, preferred_element_type=jnp.float32)


def dot_rows(left, right):
    return lax.dot_general(left, right, (((1,), (1,)), ((), ())), preferred_element_type=jnp.float32)


def split(value):
    high = value.astype(jnp.bfloat16)
    return high, (value - high.astype(jnp.float32)).astype(jnp.bfloat16)


def band_matrix():
    width = FULL + LANES
    row = lax.broadcasted_iota(jnp.int32, (width, width), 0)
    col = lax.broadcasted_iota(jnp.int32, (width, width), 1)
    out_bin = jnp.where(col < F, col, col - HALF)
    centre = jnp.clip(out_bin, SMOOTH, F - 1 - SMOOTH)
    near = (jnp.abs(row - centre) <= SMOOTH) & (row < F)
    return jnp.where(near, 1.0, 0.0).astype(jnp.bfloat16)


def whiten(signal, table, band):
    mean = jnp.sum(signal, axis=1, keepdims=True) * (1.0 / L)
    spectrum = dot((signal - mean).astype(jnp.bfloat16), table)
    real, imag, mixed = spectrum[:, :FULL], spectrum[:, FULL : 2 * FULL], spectrum[:, 2 * FULL :]
    squares = mixed * mixed
    power = jnp.concatenate([real * real + imag * imag, squares + pltpu.roll(squares, HALF, 1)], axis=1)
    amplitude = jnp.sqrt(power)
    first, rest = split(amplitude)
    second, third = split(amplitude - first.astype(jnp.float32))
    smooth = (dot(first, band) + dot(second, band) + dot(third, band)) / (2 * SMOOTH + 1)
    factor = 1.0 / (smooth + 1e-06)
    return jnp.concatenate(
        [real * factor[:, :FULL], imag * factor[:, :FULL], mixed * factor[:, FULL:]], axis=1
    )


def kernel(
    dims,
    rec_hbm,
    table_hbm,
    low_hbm,
    partners_hbm,
    counts_hbm,
    sources_hbm,
    out_ref,
    partners_ref,
    counts_ref,
    sources_ref,
    rec,
    table,
    lag_high,
    lag_low,
    band,
    white_send,
    white_recv,
    near_send,
    near_recv,
    near_rows,
    far_send,
    far_recv,
    source_full,
    source_rest,
    partner_rows,
    cross,
    stack_send,
    stack_recvs,
    local_sems,
    near_sems,
    far_sems,
    swap_sems,
    white_sems,
    stack_sems,
):
    blocks, shares, pieces, slots, sources = dims
    planes = shares // CORES
    me_chan, me_tm = lax.axis_index("chan"), lax.axis_index("tm")
    me_plane, me_core = lax.div(me_tm, CORES), lax.rem(me_tm, CORES)

    def tm_index(step, core_step):
        return lax.rem(me_plane + step, planes) * CORES + lax.rem(me_core + core_step, CORES)

    steps = sorted(range(1, planes), key=lambda step: -min(step, planes - step))
    near_peers = [("tm", tm_index(step, 0)) for step in steps]
    partner = ("tm", tm_index(0, 1))
    tm_peers = [("tm", tm_index(step, core_step)) for step in steps for core_step in range(CORES)] + [partner]
    chan_peers = [("chan", lax.rem(me_chan + step, blocks)) for step in range(1, blocks)]

    barrier = pltpu.get_barrier_semaphore()
    for axis, peer in tm_peers + chan_peers:
        pl.semaphore_signal(barrier, inc=1, device_id={axis: peer}, device_id_type=MESH)

    index_loads = [
        pltpu.make_async_copy(sources_hbm, sources_ref, local_sems.at[0]),
        pltpu.make_async_copy(partners_hbm, partners_ref, local_sems.at[1]),
        pltpu.make_async_copy(counts_hbm, counts_ref, local_sems.at[2]),
    ]
    loads = [
        pltpu.make_async_copy(rec_hbm.at[:, piece], rec.at[piece], local_sems.at[7 + piece]) for piece in range(pieces)
    ]
    table_load = pltpu.make_async_copy(table_hbm, table, local_sems.at[3])
    lag_loads = [
        pltpu.make_async_copy(table_hbm.at[pl.ds(L - HL, HL)], lag_high.at[pl.ds(0, HL)], local_sems.at[4]),
        pltpu.make_async_copy(table_hbm.at[pl.ds(0, HL)], lag_high.at[pl.ds(HL, HL)], local_sems.at[5]),
        pltpu.make_async_copy(low_hbm, lag_low, local_sems.at[6]),
    ]
    for copy in index_loads + loads + [table_load] + lag_loads:
        copy.start()

    def send(src, dst, sems, peer):
        axis, index = peer
        pltpu.make_async_remote_copy(
            src_ref=src, dst_ref=dst, send_sem=sems[0], recv_sem=sems[1], device_id={axis: index}, device_id_type=MESH
        ).start()

    def wait_bytes(ref, sem):
        pltpu.make_async_copy(ref, ref, sem).wait()

    band[...] = band_matrix()
    for copy in index_loads + loads:
        copy.wait()

    row_id = lax.broadcasted_iota(jnp.int32, (ROWS, L), 0)
    head_id = lax.broadcasted_iota(jnp.int32, (2 * ROWS, L), 0)
    head = jnp.zeros((2 * ROWS, L), jnp.float32)
    for source in range(sources):
        channel = sources_ref[0, source]
        share = lax.div(channel, pieces * ROWS)
        within = channel - share * (pieces * ROWS)
        piece = lax.div(within, ROWS)
        tile = rec[piece, share].astype(jnp.float32)
        row = jnp.sum(jnp.where(row_id == within - piece * ROWS, tile, 0.0), axis=0, keepdims=True)
        head = jnp.where(head_id == source, row, head)
    table_load.wait()
    near_send[...] = whiten(head, table[...], band[...])[:sources].astype(jnp.bfloat16).astype(jnp.float32)
    near_recv[me_plane] = near_send[...]
    pl.semaphore_wait(barrier, len(tm_peers) + len(chan_peers))
    for peer in near_peers:
        send(near_send, near_recv.at[me_plane], (near_sems.at[0], near_sems.at[1]), peer)

    for piece in range(pieces):
        white = whiten(rec[piece].astype(jnp.float32).reshape(shares * ROWS, L), table[...], band[...])
        white_send[piece] = white.reshape(shares, ROWS, COLS).astype(jnp.bfloat16)
        white_recv[piece, me_tm] = white_send[piece, me_tm]
        for peer in tm_peers:
            send(
                white_send.at[piece, peer[1]],
                white_recv.at[piece, me_tm],
                (white_sems.at[0, piece], white_sems.at[1, piece]),
                peer,
            )

    wait_bytes(near_recv.at[pl.ds(0, planes - 1)], near_sems.at[1])
    for plane in range(planes):
        for source in range(sources):
            near_rows[pl.ds(source * planes + plane, 1), :] = near_recv[plane, pl.ds(source, 1), :]
    far_send[...] = near_rows[...].astype(jnp.bfloat16)
    far_recv[me_core, me_chan] = far_send[...]
    for peer in chan_peers:
        send(far_send, far_recv.at[me_core, me_chan], (far_sems.at[0], far_sems.at[1]), peer)
    wait_bytes(far_recv.at[0, pl.ds(0, blocks - 1)], far_sems.at[1])
    send(far_recv.at[me_core], far_recv.at[me_core], (swap_sems.at[0], swap_sems.at[1]), partner)

    tiles = FULL // LANES
    lower = lax.broadcasted_iota(jnp.int32, (1, planes, LANES), 2) < HALF

    def unpack(core):
        rows = far_recv[core].astype(jnp.float32)
        for tile in range(tiles):
            real = rows[:, :, tile * LANES : (tile + 1) * LANES]
            imag = rows[:, :, (tiles + tile) * LANES : (tiles + tile + 1) * LANES]
            source_full[core, :, tile] = real
            source_full[core, :, tiles + tile] = imag
            source_full[core, :, 2 * tiles + tile] = real - imag
        first, second = rows[:, :planes, 2 * FULL :], rows[:, planes:, 2 * FULL :]
        real = jnp.where(lower, first, pltpu.roll(second, HALF, 2))
        imag = jnp.where(lower, pltpu.roll(first, HALF, 2), second)
        source_rest[core, :, 0] = real
        source_rest[core, :, 1] = imag
        source_rest[core, :, 2] = real - imag

    unpack(me_core)
    wait_bytes(far_recv.at[0], swap_sems.at[1])
    unpack(1 - me_core)

    for copy in lag_loads:
        copy.wait()
    lane_low = lax.broadcasted_iota(jnp.int32, (ROWS, LANES), 1) < HALF
    scale = 1.0 / math.sqrt(F * shares)

    def products(reals, imags, sums, a_real, a_imag, a_diff, b_real, b_imag, b_sum):
        return reals + a_real * b_real, imags + a_imag * b_imag, sums + a_diff * b_sum

    for piece in range(pieces):
        wait_bytes(white_recv.at[piece, pl.ds(0, shares - 1)], white_sems.at[1, piece])
        spectra = white_recv[piece].astype(jnp.float32)
        real, imag = spectra[:, :, :FULL], spectra[:, :, FULL : 2 * FULL]
        mixed = spectra[:, :, 2 * FULL :]
        turned = pltpu.roll(mixed, HALF, 2)
        rest_low = lax.broadcasted_iota(jnp.int32, mixed.shape, 2) < HALF
        rest_real, rest_imag = jnp.where(rest_low, mixed, turned), jnp.where(rest_low, turned, mixed)
        partner_rows[:, :, : 2 * FULL] = spectra[:, :, : 2 * FULL]
        partner_rows[:, :, 2 * FULL : 3 * FULL] = real + imag
        for index, value in enumerate((rest_real, rest_imag, rest_real + rest_imag)):
            partner_rows[:, :, 3 * FULL + index * LANES : 3 * FULL + (index + 1) * LANES] = value

        def some_blocks(group, carry):
            members = [group * TOGETHER + member for member in range(TOGETHER)]

            def partner_tile(window, tile):
                return partner_rows[window, :, pl.ds(tile * LANES, LANES)]

            for tile in range(tiles):
                totals = {(m, s): (0.0, 0.0, 0.0) for m in range(TOGETHER) for s in range(sources)}
                for window in range(shares):
                    plane, core = window // CORES, window % CORES
                    b_tiles = [partner_tile(window, kind * tiles + tile) for kind in range(3)]
                    for m, s in totals:
                        a_tiles = [
                            source_full[
                                core, members[m], kind * tiles + tile, pl.ds(s * planes + plane, ROWS, stride=0), :
                            ]
                            for kind in range(3)
                        ]
                        totals[m, s] = products(*totals[m, s], *a_tiles, *b_tiles)
                for (m, s), (reals, imags, sums) in totals.items():
                    row = members[m] * sources + s
                    cross[row, :, pl.ds(tile * LANES, LANES)] = reals + imags
                    cross[row, :, pl.ds((tiles + tile) * LANES, LANES)] = sums - reals + imags
            rest = [(0.0, 0.0, 0.0)] * TOGETHER
            for window in range(shares):
                plane, core = window // CORES, window % CORES
                b_tiles = [partner_tile(window, 3 * tiles + kind) for kind in range(3)]
                for m in range(TOGETHER):
                    a_tiles = [source_rest[core, members[m], kind, pl.ds(plane, ROWS, stride=0), :] for kind in range(3)]
                    rest[m] = products(*rest[m], *a_tiles, *b_tiles)
            for m, (reals, imags, sums) in enumerate(rest):
                real_part, imag_part = reals + imags, sums - reals + imags
                columns = pl.ds(2 * FULL, LANES)
                cross[members[m] * sources, :, columns] = jnp.where(
                    lane_low, real_part, pltpu.roll(imag_part, HALF, 1)
                )
                cross[members[m] * sources + 1, :, columns] = jnp.where(
                    lane_low, pltpu.roll(real_part, HALF, 1), imag_part
                )
            return carry

        lax.fori_loop(0, blocks // TOGETHER, some_blocks, 0)
        high, low = split(cross[...].reshape(blocks * sources * ROWS, COLS))
        lagged = dot_rows(high, lag_high[...]) + dot_rows(low, lag_high[...]) + dot_rows(high, lag_low[...])
        stack_send[piece] = (lagged * scale).reshape(blocks, sources, ROWS, 2 * HL).astype(jnp.bfloat16)
        stack_recvs[piece][me_chan] = stack_send[piece, me_chan]
        for peer in chan_peers:
            send(
                stack_send.at[piece, peer[1]],
                stack_recvs[piece].at[me_chan],
                (stack_sems.at[0, piece], stack_sems.at[1, piece]),
                peer,
            )

    for piece in range(pieces):
        wait_bytes(stack_recvs[piece].at[pl.ds(0, blocks - 1)], stack_sems.at[1, piece])
        for slot in range(slots):
            stack = stack_recvs[piece][partners_ref[0, slot]].astype(jnp.float32)
            out_ref[slot, :, pl.ds(piece * ROWS, ROWS), :] = jnp.where(slot < counts_ref[0], stack, 0.0)

    wait_bytes(near_recv.at[pl.ds(0, planes - 1)], near_sems.at[0])
    wait_bytes(far_recv.at[0, pl.ds(0, blocks - 1)], far_sems.at[0])
    wait_bytes(far_recv.at[0], swap_sems.at[0])
    for piece in range(pieces):
        wait_bytes(white_recv.at[piece, pl.ds(0, shares - 1)], white_sems.at[0, piece])
        wait_bytes(stack_recvs[piece].at[pl.ds(0, blocks - 1)], stack_sems.at[0, piece])


def local(blocks, shares, records, partners, counts, sources):
    channels = records.shape[1]
    slots, picks = partners.shape[1], sources.shape[1]
    pieces = channels // (shares * ROWS)
    high, low = tables()
    bf16, f32 = jnp.bfloat16, jnp.float32
    planes, tiles = shares // CORES, FULL // LANES
    result = pl.pallas_call(
        functools.partial(kernel, (blocks, shares, pieces, slots, picks)),
        out_shape=jax.ShapeDtypeStruct((slots, picks, pieces * ROWS, 2 * HL), f32),
        in_specs=[pl.BlockSpec(memory_space=pl.ANY)] * 6,
        out_specs=pl.BlockSpec(memory_space=pltpu.VMEM),
        scratch_shapes=[
            pltpu.SMEM((1, slots), jnp.int32),
            pltpu.SMEM((1,), jnp.int32),
            pltpu.SMEM((1, picks), jnp.int32),
            pltpu.VMEM((pieces, shares, ROWS, L), bf16),
            pltpu.VMEM((L, COLS), bf16),
            pltpu.VMEM((2 * HL, COLS), bf16),
            pltpu.VMEM((2 * HL, COLS), bf16),
            pltpu.VMEM((FULL + LANES, FULL + LANES), bf16),
            pltpu.VMEM((pieces, shares, ROWS, COLS), bf16),
            pltpu.VMEM((pieces, shares, ROWS, COLS), bf16),
            pltpu.VMEM((picks, COLS), f32),
            pltpu.VMEM((planes, picks, COLS), f32),
            pltpu.VMEM((planes * picks, COLS), f32),
            pltpu.VMEM((planes * picks, COLS), bf16),
            pltpu.VMEM((CORES, blocks, planes * picks, COLS), bf16),
            pltpu.VMEM((CORES, blocks, 3 * tiles, planes * picks, LANES), f32),
            pltpu.VMEM((CORES, blocks, 3, planes, LANES), f32),
            pltpu.VMEM((shares, ROWS, 3 * FULL + 3 * LANES), f32),
            pltpu.VMEM((blocks * picks, ROWS, COLS), f32),
            pltpu.VMEM((pieces, blocks, picks, ROWS, 2 * HL), bf16),
            [pltpu.VMEM((blocks, picks, ROWS, 2 * HL), bf16) for _ in range(pieces)],
            pltpu.SemaphoreType.DMA((7 + pieces,)),
            pltpu.SemaphoreType.DMA((2,)),
            pltpu.SemaphoreType.DMA((2,)),
            pltpu.SemaphoreType.DMA((2,)),
            pltpu.SemaphoreType.DMA((2, pieces)),
            pltpu.SemaphoreType.DMA((2, pieces)),
        ],
        compiler_params=pltpu.CompilerParams(
            collective_id=0, has_side_effects=True, vmem_limit_bytes=67_043_328
        ),
        name="correlate",
    )(
        records.reshape(shares, pieces, ROWS, L),
        jnp.asarray(high),
        jnp.asarray(low),
        partners,
        counts,
        sources,
    )
    return result.transpose(2, 0, 1, 3)[None]


def solution(mesh):
    return jax.shard_map(
        functools.partial(local, mesh.shape["chan"], mesh.shape["tm"]),
        mesh=mesh,
        in_specs=(P("tm", "chan", None), P("chan", None), P("chan"), P("chan", None)),
        out_specs=P("chan", "tm", None, None, None),
        check_vma=False,
    )
```
